32 devices in a mesh: lat: 8 (over y, x, core), lon: 4 (over z).
Axes of the slice: x: 2, y: 2, z: 4, core: 2. Of those that a mesh axis runs over, the one named last changes fastest.
Arguments:
- tracer: float32 [16, 64, 2880], P(None, 'lat', 'lon'), may hold values from -6 to 6
- zonal_courant: float32 [16, 64, 2880], P(None, 'lat', 'lon'), may hold values from -0.35 to 0.35
- north_courant: float32 [16, 64, 2880], P(None, 'lat', 'lon'), may hold values from -0.35 to 0.35
- cutoff: int32 [16], replicated, may hold values from 1 to 128
Outputs:
- advanced: float32 [16, 64, 2880], P(None, 'lat', 'lon')
The draws below stay inside these ranges and needn't reach their ends.
All inputs are finite; a program needn't handle non-finite values.
Results may differ from the reference program's by a relative error of at most 0.0001.
Values sent between devices are 32-bit elements; how exact they have to be, the bound alone decides.
A program may use at most 64 MiB of HBM per device.

```python
import jax
import jax.numpy as jnp

NLON = 2880
KMAX = 128
LEV = 16
NLAT = 64
CAP_ROWS = 8


def set_ends(values, key, low, high):
    index_at = [jax.random.randint(jax.random.fold_in(key, axis), (), 0, length) for axis, length in enumerate(values.shape)]
    main_axis = values.shape.index(max(values.shape))
    beside = index_at[:main_axis] + [(index_at[main_axis] + 1) % values.shape[main_axis]] + index_at[main_axis + 1:]
    return values.at[tuple(index_at)].set(low).at[tuple(beside)].set(high)


def levels(stream_key, extent, cuts, low, largest):
    def one(dim, blocks):
        steps = jax.random.uniform(jax.random.fold_in(jax.random.fold_in(stream_key, 6), dim), (blocks,), jnp.float32, low / len(cuts), largest / len(cuts))
        return jnp.repeat(jnp.exp(steps), extent[dim] // blocks).reshape((-1,) + (1,) * (len(extent) - dim - 1))

    loudness = one(*cuts[0])
    for cut in cuts[1:]:
        loudness = loudness * one(*cut)
    return loudness


def centred(own_key, shape, deviation, bound, shards=(), held_as=jnp.bfloat16):
    gain = levels(own_key, shape, shards, -0.22, 0.18) if shards else 1.0
    drawn = jax.random.normal(own_key, shape, jnp.float32) * deviation * gain
    return jnp.minimum(jnp.maximum(drawn, -bound), bound).astype(held_as)


def setup_inputs(seed: int = 0) -> dict:
    key_of = jax.random.split(jax.random.key(seed), 5)
    return {
        "tracer": centred(key_of[0], (LEV, NLAT, NLON), 1.0, 6.0, ((1, 8), (2, 4)), jnp.float32),
        "zonal_courant": jnp.clip(jax.random.uniform(key_of[1], (LEV, NLAT, NLON), jnp.float32, -0.35, 0.35) * levels(key_of[1], (LEV, NLAT, NLON), ((1, 8), (2, 4)), -0.4, 0.0), -0.35, 0.35),
        "north_courant": jnp.clip(jax.random.uniform(key_of[2], (LEV, NLAT, NLON), jnp.float32, -0.35, 0.35) * levels(key_of[2], (LEV, NLAT, NLON), ((1, 8), (2, 4)), -0.4, 0.0), -0.35, 0.35),
        "cutoff": set_ends(jax.random.randint(key_of[3], (2 * CAP_ROWS,), 1, KMAX + 1), jax.random.fold_in(key_of[3], 1), 1, KMAX).astype(jnp.int32),
    }


DIFFUSION = 0.2


def tendency_of(tracer, zonal_courant, north_courant):
    half_turn = NLON // 2
    south_edge = jnp.roll(tracer[:, :1], half_turn, axis=2)
    north_edge = jnp.roll(tracer[:, -1:], half_turn, axis=2)
    padded = jnp.concatenate([south_edge, tracer, north_edge], axis=1)
    south_cell = padded[:, :-2]
    north_cell = padded[:, 2:]
    east_cell = jnp.roll(tracer, -1, axis=2)
    west_cell = jnp.roll(tracer, 1, axis=2)
    return (-0.5 * zonal_courant * (east_cell - west_cell)
            - 0.5 * north_courant * (north_cell - south_cell)
            + DIFFUSION * (east_cell + west_cell + north_cell + south_cell - 4.0 * tracer))


def polar_filter(rows_block, cut_rows):
    spectrum = jnp.fft.rfft(rows_block, axis=-1)
    modes = jnp.arange(spectrum.shape[-1], dtype=jnp.int32)
    kept_modes = modes[None, None, :] < cut_rows[None, :, None]
    spectrum = jnp.where(kept_modes, spectrum, jnp.zeros_like(spectrum))
    return jnp.fft.irfft(spectrum, n=NLON, axis=-1).astype(jnp.float32)


def reference(tracer, zonal_courant, north_courant, cutoff):
    cap_rows = CAP_ROWS
    state = tracer
    for substep in range(2):
        tendency = tendency_of(state, zonal_courant, north_courant)
        south_part = polar_filter(tendency[:, :cap_rows], cutoff[:cap_rows])
        north_part = polar_filter(tendency[:, -cap_rows:], cutoff[cap_rows:])
        tendency = jnp.concatenate([south_part, tendency[:, cap_rows:-cap_rows], north_part], axis=1)
        state = state + tendency
    return state
```

```python
import functools
import math

import jax
import jax.numpy as jnp
import numpy as np
from jax import lax
from jax.experimental import pallas as pl
from jax.experimental.pallas import tpu as pltpu
from jax.sharding import PartitionSpec as P

KMAX = 128
DIFFUSION = 0.2
LANES = 128
MESH = pl.DeviceIdType.MESH
F32 = jnp.float32
BF16 = jnp.bfloat16


def split_table(table):
    high = table.astype(np.float32).astype(BF16)
    low = (table - high.astype(np.float64)).astype(np.float32).astype(BF16)
    return np.stack([high, low])


def tables(cols, width, lon_count):
    lane = np.arange(width)
    lane = np.where(lane == width - 1, -1, lane)
    modes = np.arange(KMAX)
    total = cols * lon_count
    angle = (lane[:, None] * modes[None, :] % total) * (2.0 * math.pi / total)
    both = np.concatenate([np.cos(angle), np.sin(angle)], axis=1)
    block = np.arange(lon_count) * cols
    turn = (block[:, None] * modes[None, :] % total) * (2.0 * math.pi / total)
    phase = np.zeros((lon_count, 8, KMAX), np.float32)
    phase[:, 0] = np.cos(turn)
    phase[:, 1] = np.sin(turn)
    return split_table(both), split_table(both.T.copy()), phase


def split(value):
    high = value.astype(BF16)
    low = (value - high.astype(F32)).astype(BF16)
    return high, low


def dot3(value, table):
    high, low = split(value)
    t_high = table[0]
    t_low = table[1]
    dot = functools.partial(jnp.dot, preferred_element_type=F32)
    return dot(high, t_high) + (dot(low, t_high) + dot(high, t_low))


def kernel(
    lat_count, lon_count, cap_blocks,
    cut_ref, tracer, zonal, north, ana_hbm, syn_hbm, phase_hbm, out_hbm,
    q_in, zc, nc, ana, syn, phase, out, q, tend,
    row_out, row_in, col_out, col_in, pole_in,
    part, part_in, coef,
    load_sem, row_send, row_recv, col_send, col_recv, pole_send, pole_recv,
    rs_send, rs_recv, ag_send, ag_recv,
):
    levels, rows, cols = q_in.shape
    width = q.shape[2]
    total = cols * lon_count
    per = levels // lon_count
    lat = lax.axis_index("lat")
    lon = lax.axis_index("lon")
    polar = jnp.logical_or(lat < cap_blocks, lat >= lat_count - cap_blocks)
    first = lat == 0
    last = lat == lat_count - 1
    east = lax.rem(lon + 1, lon_count)
    west = lax.rem(lon + lon_count - 1, lon_count)
    across = lax.rem(lon + lon_count // 2, lon_count)

    loads = [
        pltpu.make_async_copy(tracer, q_in, load_sem.at[0]),
        pltpu.make_async_copy(zonal, zc, load_sem.at[1]),
        pltpu.make_async_copy(north, nc, load_sem.at[2]),
        pltpu.make_async_copy(ana_hbm, ana, load_sem.at[3]),
        pltpu.make_async_copy(syn_hbm, syn, load_sem.at[4]),
        pltpu.make_async_copy(phase_hbm.at[lon], phase, load_sem.at[5]),
    ]
    for load in loads:
        load.start()

    barrier = pltpu.get_barrier_semaphore()

    def greet(there):
        pl.semaphore_signal(barrier, inc=1, device_id=there, device_id_type=MESH)

    @pl.when(jnp.logical_not(first))
    def _():
        greet({"lat": lat - 1, "lon": lon})

    @pl.when(jnp.logical_not(last))
    def _():
        greet({"lat": lat + 1, "lon": lon})

    @pl.when(polar)
    def _():
        for step in range(1, lon_count):
            greet({"lat": lat, "lon": lax.rem(lon + step, lon_count)})

    @pl.when(jnp.logical_not(polar))
    def _():
        greet({"lat": lat, "lon": east})
        greet({"lat": lat, "lon": west})

    lane = lax.broadcasted_iota(jnp.int32, (rows, LANES), 1)
    row_at = lax.broadcasted_iota(jnp.int32, (rows, width), 0)

    def row_copy(turn, side):
        there = lat + 1 if side == 0 else lat - 1
        return pltpu.make_async_remote_copy(
            row_out.at[turn, side], row_in.at[turn, side],
            row_send.at[turn, side], row_recv.at[turn, side],
            device_id={"lat": there, "lon": lon}, device_id_type=MESH)

    def col_copy(turn, side):
        return pltpu.make_async_remote_copy(
            col_out.at[turn, side], col_in.at[turn, side],
            col_send.at[turn, side], col_recv.at[turn, side],
            device_id={"lat": lat, "lon": east if side == 0 else west}, device_id_type=MESH)

    def pole_copy(side):
        return pltpu.make_async_remote_copy(
            row_out.at[0, side], pole_in, pole_send, pole_recv,
            device_id={"lat": lat, "lon": across}, device_id_type=MESH)

    def rs_copy(turn, step):
        there = lax.rem(lon + step, lon_count)
        return pltpu.make_async_remote_copy(
            part.at[turn, pl.ds(there * per, per)], part_in.at[turn, step - 1],
            rs_send.at[turn, step - 1], rs_recv.at[turn, step - 1],
            device_id={"lat": lat, "lon": there}, device_id_type=MESH)

    def ag_copy(turn, step):
        there = lax.rem(lon + step, lon_count)
        mine = coef.at[turn, pl.ds(lon * per, per)]
        return pltpu.make_async_remote_copy(
            mine, mine, ag_send.at[turn, step - 1], ag_recv.at[turn, step - 1],
            device_id={"lat": lat, "lon": there}, device_id_type=MESH)

    def ag_arrival(turn, step):
        origin = lax.rem(lon + lon_count - step, lon_count)
        theirs = coef.at[turn, pl.ds(origin * per, per)]
        return pltpu.make_async_remote_copy(
            theirs, theirs, ag_send.at[turn, step - 1], ag_recv.at[turn, step - 1],
            device_id={"lat": lat, "lon": origin}, device_id_type=MESH)

    def pack_rows(turn):
        row_out[turn, 0] = q[:, rows - 1, :]
        row_out[turn, 1] = q[:, 0, :]

    def pack_cols(turn):
        end_tile = (cols - 1) // LANES * LANES
        high = jnp.zeros((rows, LANES), F32)
        low = jnp.zeros((rows, LANES), F32)
        for level in range(levels):
            tile = q[level, :, end_tile:end_tile + LANES]
            high = jnp.where(lane == level, pltpu.roll(tile, (level - (cols - 1) % LANES) % LANES, 1), high)
            tile = q[level, :, 0:LANES]
            low = jnp.where(lane == level, pltpu.roll(tile, level, 1) if level else tile, low)
        col_out[turn, 0] = high
        col_out[turn, 1] = low

    def place_cols(turn):
        from_west = col_in[turn, 0]
        from_east = col_in[turn, 1]
        east_tile = cols // LANES * LANES
        west_tile = width - LANES
        for level in range(levels):
            tile = q[level, :, east_tile:east_tile + LANES]
            moved = pltpu.roll(from_east, (cols % LANES - level) % LANES, 1)
            q[level, :, east_tile:east_tile + LANES] = jnp.where(lane == cols % LANES, moved, tile)
            tile = q[level, :, west_tile:west_tile + LANES]
            moved = pltpu.roll(from_west, (LANES - 1 - level) % LANES, 1)
            q[level, :, west_tile:west_tile + LANES] = jnp.where(lane == LANES - 1, moved, tile)

    def stencil(turn, level):
        here = q[level]
        to_east = pltpu.roll(here, width - 1, 1)
        to_west = pltpu.roll(here, 1, 1)
        top = row_in[turn, 1, pl.ds(level, 1), :]
        bottom = row_in[turn, 0, pl.ds(level, 1), :]
        to_north = jnp.where(row_at == rows - 1, top, pltpu.roll(here, rows - 1, 0))
        to_south = jnp.where(row_at == 0, bottom, pltpu.roll(here, 1, 0))
        here, to_east, to_west, to_north, to_south = (
            value[:, :cols] for value in (here, to_east, to_west, to_north, to_south))
        return (-0.5 * zc[level] * (to_east - to_west)
                - 0.5 * nc[level] * (to_north - to_south)
                + DIFFUSION * (to_east + to_west + to_north + to_south - 4.0 * here))

    q[:, :, (width - LANES):] = jnp.zeros((levels, rows, LANES), F32)
    loads[0].wait()
    for level in range(levels):
        q[level, :, :cols] = q_in[level]
    pack_rows(0)
    pack_cols(0)

    ends = first.astype(jnp.int32) + last.astype(jnp.int32)
    sides = jnp.where(polar, lon_count - 1, 2)
    pl.semaphore_wait(barrier, 2 - ends + sides)

    @pl.when(jnp.logical_not(last))
    def _():
        row_copy(0, 0).start()

    @pl.when(jnp.logical_not(first))
    def _():
        row_copy(0, 1).start()

    @pl.when(last)
    def _():
        pole_copy(0).start()

    @pl.when(first)
    def _():
        pole_copy(1).start()

    col_copy(0, 0).start()
    col_copy(0, 1).start()

    offset = jnp.where(
        lat < cap_blocks, lat * rows,
        jnp.where(polar, (lat - lat_count + 2 * cap_blocks) * rows, 0))
    tend[...] = jnp.zeros_like(tend)
    for load in loads[1:]:
        load.wait()

    @pl.when(jnp.logical_not(last))
    def _():
        row_copy(0, 1).wait_recv()
        row_copy(0, 0).wait_send()

    @pl.when(jnp.logical_not(first))
    def _():
        row_copy(0, 0).wait_recv()
        row_copy(0, 1).wait_send()

    @pl.when(last)
    def _():
        pole_copy(0).wait()
        row_in[0, 1] = pole_in[...]

    @pl.when(first)
    def _():
        pole_copy(1).wait()
        row_in[0, 0] = pole_in[...]

    col_copy(0, 0).wait()
    col_copy(0, 1).wait()
    place_cols(0)

    @pl.when(jnp.logical_not(polar))
    def _():
        for level in range(levels):
            tend[level, :, :cols] = stencil(0, level)
        for level in range(levels):
            q[level, :, :cols] = q[level, :, :cols] + tend[level, :, :cols]
        pack_rows(1)
        row_copy(1, 0).start()
        row_copy(1, 1).start()
        pack_cols(1)
        col_copy(1, 0).start()
        col_copy(1, 1).start()
        row_copy(1, 0).wait()
        row_copy(1, 1).wait()
        col_copy(1, 0).wait()
        col_copy(1, 1).wait()
        place_cols(1)
        for level in range(levels):
            out[level] = q[level, :, :cols] + stencil(1, level)

    @pl.when(polar)
    def _():
        mode = lax.broadcasted_iota(jnp.int32, (rows, KMAX), 1)
        which = lax.broadcasted_iota(jnp.int32, (rows, KMAX), 0)
        weight = jnp.where(mode == 0, 1.0 / total, 2.0 / total).astype(F32)
        cut = jnp.zeros((rows, KMAX), jnp.int32)
        for row in range(rows):
            cut = jnp.where(which == row, cut_ref[offset + row], cut)
        keep = jnp.where(mode < cut, weight, 0.0)[None]
        cosine = phase[0:1, :]
        sine = phase[1:2, :]
        parity = 1.0 - 2.0 * (lax.broadcasted_iota(jnp.int32, (1, 2 * KMAX), 1) % 2).astype(F32)

        def filtered_coefficients(turn):
            partial = dot3(tend[...].reshape(levels * rows, width), ana)
            real = partial[:, :KMAX]
            imag = partial[:, KMAX:]
            part[turn, :, :, :KMAX] = (real * cosine - imag * sine).reshape(levels, rows, KMAX)
            part[turn, :, :, KMAX:] = (real * sine + imag * cosine).reshape(levels, rows, KMAX)
            for step in range(1, lon_count):
                rs_copy(turn, step).start()
            summed = part[turn, pl.ds(lon * per, per)]
            for step in range(1, lon_count):
                rs_copy(turn, step).wait_recv()
                summed = summed + part_in[turn, step - 1]
            coef[turn, pl.ds(lon * per, per), :, :KMAX] = summed[:, :, :KMAX] * keep
            coef[turn, pl.ds(lon * per, per), :, KMAX:] = summed[:, :, KMAX:] * keep
            for step in range(1, lon_count):
                ag_copy(turn, step).start()
            for step in range(1, lon_count):
                rs_copy(turn, step).wait_send()
            for step in range(1, lon_count):
                ag_arrival(turn, step).wait_recv()
            for step in range(1, lon_count):
                ag_copy(turn, step).wait_send()
            sums = coef[turn].reshape(levels * rows, 2 * KMAX)
            real = sums[:, :KMAX]
            imag = sums[:, KMAX:]
            return jnp.concatenate(
                [real * cosine + imag * sine, imag * cosine - real * sine], axis=1)

        for level in range(levels):
            tend[level, :, :cols] = stencil(0, level)
        local = filtered_coefficients(0)
        filtered = dot3(local, syn)
        q[...] = q[...] + filtered.reshape(levels, rows, width)
        pack_rows(1)

        @pl.when(jnp.logical_not(last))
        def _():
            row_copy(1, 0).start()

        @pl.when(jnp.logical_not(first))
        def _():
            row_copy(1, 1).start()

        by_level = local.reshape(levels, rows, 2 * KMAX)
        pole_row = jnp.where(first, by_level[:, 0, :], by_level[:, rows - 1, :]) * parity
        pole_sum = pole_in[...] + dot3(pole_row, syn)

        @pl.when(last)
        def _():
            row_in[1, 1] = pole_sum

        @pl.when(first)
        def _():
            row_in[1, 0] = pole_sum

        @pl.when(jnp.logical_not(last))
        def _():
            row_copy(1, 1).wait_recv()
            row_copy(1, 0).wait_send()

        @pl.when(jnp.logical_not(first))
        def _():
            row_copy(1, 0).wait_recv()
            row_copy(1, 1).wait_send()

        for level in range(levels):
            tend[level, :, :cols] = stencil(1, level)
        filtered = dot3(filtered_coefficients(1), syn)
        filtered = filtered.reshape(levels, rows, width)
        for level in range(levels):
            out[level] = q[level, :, :cols] + filtered[level, :, :cols]

    store = pltpu.make_async_copy(out, out_hbm, load_sem.at[0])
    store.start()
    store.wait()


def shards(tracer, zonal_courant, north_courant, cutoff):
    levels, rows, cols = tracer.shape
    lat_count = lax.axis_size("lat")
    lon_count = lax.axis_size("lon")
    cap_blocks = lat_count // 8
    width = -(-(cols + 2) // LANES) * LANES
    per = levels // lon_count
    analysis, synthesis, phase = tables(cols, width, lon_count)
    peers = lon_count - 1
    dma = pltpu.SemaphoreType.DMA
    anywhere = pl.BlockSpec(memory_space=pl.ANY)
    return pl.pallas_call(
        functools.partial(kernel, lat_count, lon_count, cap_blocks),
        out_shape=jax.ShapeDtypeStruct(tracer.shape, F32),
        in_specs=[pl.BlockSpec(memory_space=pltpu.SMEM)] + [anywhere] * 6,
        out_specs=anywhere,
        scratch_shapes=[
            pltpu.VMEM((levels, rows, cols), F32),
            pltpu.VMEM((levels, rows, cols), F32),
            pltpu.VMEM((levels, rows, cols), F32),
            pltpu.VMEM(analysis.shape, BF16),
            pltpu.VMEM(synthesis.shape, BF16),
            pltpu.VMEM(phase.shape[1:], F32),
            pltpu.VMEM((levels, rows, cols), F32),
            pltpu.VMEM((levels, rows, width), F32),
            pltpu.VMEM((levels, rows, width), F32),
            pltpu.VMEM((2, 2, levels, width), F32),
            pltpu.VMEM((2, 2, levels, width), F32),
            pltpu.VMEM((2, 2, rows, LANES), F32),
            pltpu.VMEM((2, 2, rows, LANES), F32),
            pltpu.VMEM((levels, width), F32),
            pltpu.VMEM((2, levels, rows, 2 * KMAX), F32),
            pltpu.VMEM((2, peers, per, rows, 2 * KMAX), F32),
            pltpu.VMEM((2, levels, rows, 2 * KMAX), F32),
            dma((6,)),
            dma((2, 2)), dma((2, 2)), dma((2, 2)), dma((2, 2)),
            dma(()), dma(()),
            dma((2, peers)), dma((2, peers)), dma((2, peers)), dma((2, peers)),
        ],
        compiler_params=pltpu.CompilerParams(collective_id=0, has_side_effects=True),
    )(cutoff, tracer, zonal_courant, north_courant,
      jnp.asarray(analysis), jnp.asarray(synthesis), jnp.asarray(phase))


def solution(mesh):
    return jax.shard_map(
        shards,
        mesh=mesh,
        in_specs=(P(None, "lat", "lon"), P(None, "lat", "lon"), P(None, "lat", "lon"), P()),
        out_specs=P(None, "lat", "lon"),
        check_vma=False,
    )
```

```python
import functools
import math

import jax
import jax.numpy as jnp
import numpy as np
from jax import lax
from jax.experimental import pallas as pl
from jax.experimental.pallas import tpu as pltpu
from jax.sharding import PartitionSpec as P

KMAX = 128
DIFFUSION = 0.2
PIECES = 1
LANES = 128
MESH = pl.DeviceIdType.MESH
F32 = jnp.float32
BF16 = jnp.bfloat16


def split_table(table):
    high = table.astype(np.float32).astype(BF16)
    low = (table - high.astype(np.float64)).astype(np.float32).astype(BF16)
    return np.stack([high, low])


def tables(cols, width, lon_count):
    lane = np.arange(width)
    lane = np.where(lane == width - 1, -1, lane)
    modes = np.arange(KMAX)
    total = cols * lon_count
    angle = (lane[:, None] * modes[None, :] % total) * (2.0 * math.pi / total)
    both = np.concatenate([np.cos(angle), np.sin(angle)], axis=1)
    block = np.arange(lon_count) * cols
    turn = (block[:, None] * modes[None, :] % total) * (2.0 * math.pi / total)
    phase = np.zeros((lon_count, 8, KMAX), np.float32)
    phase[:, 0] = np.cos(turn)
    phase[:, 1] = np.sin(turn)
    return split_table(both), split_table(both.T.copy()), phase


def split(value):
    high = value.astype(BF16)
    low = (value - high.astype(F32)).astype(BF16)
    return high, low


def dot3(value, table):
    high, low = split(value)
    t_high = table[0]
    t_low = table[1]
    dot = functools.partial(jnp.dot, preferred_element_type=F32)
    return dot(high, t_high) + (dot(low, t_high) + dot(high, t_low))


def kernel(
    lat_count, lon_count, cap_blocks,
    cut_ref, tracer, zonal, north, ana_hbm, syn_hbm, phase_hbm, out,
    q_in, zc, nc, ana, syn, phase, q, tend,
    row_out, row_in, col_out, col_in, pole_in,
    part, part_in,
    load_sem, row_send, row_recv, col_send, col_recv, pole_send, pole_recv,
    sum_send, sum_recv,
):
    levels, rows, cols = q_in.shape
    width = q.shape[2]
    total = cols * lon_count
    per = levels // PIECES
    lat = lax.axis_index("lat")
    lon = lax.axis_index("lon")
    polar = jnp.logical_or(lat < cap_blocks, lat >= lat_count - cap_blocks)
    first = lat == 0
    last = lat == lat_count - 1
    east = lax.rem(lon + 1, lon_count)
    west = lax.rem(lon + lon_count - 1, lon_count)
    across = lax.rem(lon + lon_count // 2, lon_count)

    loads = [
        pltpu.make_async_copy(tracer, q_in, load_sem.at[0]),
        pltpu.make_async_copy(zonal, zc, load_sem.at[1]),
        pltpu.make_async_copy(north, nc, load_sem.at[2]),
        pltpu.make_async_copy(ana_hbm, ana, load_sem.at[3]),
        pltpu.make_async_copy(syn_hbm, syn, load_sem.at[4]),
        pltpu.make_async_copy(phase_hbm.at[lon], phase, load_sem.at[5]),
    ]
    loads[0].start()

    barrier = pltpu.get_barrier_semaphore()

    def greet(there):
        pl.semaphore_signal(barrier, inc=1, device_id=there, device_id_type=MESH)

    @pl.when(jnp.logical_not(first))
    def _():
        greet({"lat": lat - 1, "lon": lon})

    @pl.when(jnp.logical_not(last))
    def _():
        greet({"lat": lat + 1, "lon": lon})

    @pl.when(polar)
    def _():
        for step in range(1, lon_count):
            greet({"lat": lat, "lon": lax.rem(lon + step, lon_count)})

    @pl.when(jnp.logical_not(polar))
    def _():
        greet({"lat": lat, "lon": east})
        greet({"lat": lat, "lon": west})

    lane = lax.broadcasted_iota(jnp.int32, (rows, LANES), 1)
    row_at = lax.broadcasted_iota(jnp.int32, (rows, width), 0)

    def row_copy(turn, side):
        there = lat + 1 if side == 0 else lat - 1
        return pltpu.make_async_remote_copy(
            row_out.at[turn, side], row_in.at[turn, side],
            row_send.at[turn, side], row_recv.at[turn, side],
            device_id={"lat": there, "lon": lon}, device_id_type=MESH)

    def col_copy(turn, side):
        return pltpu.make_async_remote_copy(
            col_out.at[turn, side], col_in.at[turn, side],
            col_send.at[turn, side], col_recv.at[turn, side],
            device_id={"lat": lat, "lon": east if side == 0 else west}, device_id_type=MESH)

    def pole_copy(side):
        return pltpu.make_async_remote_copy(
            row_out.at[0, side], pole_in, pole_send, pole_recv,
            device_id={"lat": lat, "lon": across}, device_id_type=MESH)

    def sum_copy(turn, piece, target):
        return pltpu.make_async_remote_copy(
            part.at[turn, pl.ds(piece * per, per)], part_in.at[turn, lon, pl.ds(piece * per, per)],
            sum_send.at[turn, piece, target], sum_recv.at[turn, piece, lon],
            device_id={"lat": lat, "lon": target}, device_id_type=MESH)

    def sum_arrival(turn, piece, source):
        theirs = part_in.at[turn, source, pl.ds(piece * per, per)]
        return pltpu.make_async_remote_copy(
            theirs, theirs, sum_send.at[turn, piece, source], sum_recv.at[turn, piece, source],
            device_id={"lat": lat, "lon": source}, device_id_type=MESH)

    def send_sums(turn, piece):
        for distance in range(lon_count - 1, 0, -1):
            @pl.when(lon + distance < lon_count)
            def _():
                sum_copy(turn, piece, lon + distance).start()

            @pl.when(lon - distance >= 0)
            def _():
                sum_copy(turn, piece, lon - distance).start()

    def pack_rows(turn):
        row_out[turn, 0] = q[:, rows - 1, :]
        row_out[turn, 1] = q[:, 0, :]

    def pack_cols(turn):
        end_tile = (cols - 1) // LANES * LANES
        high = jnp.zeros((rows, LANES), F32)
        low = jnp.zeros((rows, LANES), F32)
        for level in range(levels):
            tile = q[level, :, end_tile:end_tile + LANES]
            high = jnp.where(lane == level, pltpu.roll(tile, (level - (cols - 1) % LANES) % LANES, 1), high)
            tile = q[level, :, 0:LANES]
            low = jnp.where(lane == level, pltpu.roll(tile, level, 1) if level else tile, low)
        col_out[turn, 0] = high
        col_out[turn, 1] = low

    def place_cols(turn):
        from_west = col_in[turn, 0]
        from_east = col_in[turn, 1]
        east_tile = cols // LANES * LANES
        west_tile = width - LANES
        for level in range(levels):
            tile = q[level, :, east_tile:east_tile + LANES]
            moved = pltpu.roll(from_east, (cols % LANES - level) % LANES, 1)
            q[level, :, east_tile:east_tile + LANES] = jnp.where(lane == cols % LANES, moved, tile)
            tile = q[level, :, west_tile:west_tile + LANES]
            moved = pltpu.roll(from_west, (LANES - 1 - level) % LANES, 1)
            q[level, :, west_tile:west_tile + LANES] = jnp.where(lane == LANES - 1, moved, tile)

    def stencil(turn, level):
        here = q[level]
        to_east = pltpu.roll(here, width - 1, 1)
        to_west = pltpu.roll(here, 1, 1)
        top = row_in[turn, 1, pl.ds(level, 1), :]
        bottom = row_in[turn, 0, pl.ds(level, 1), :]
        to_north = jnp.where(row_at == rows - 1, top, pltpu.roll(here, rows - 1, 0))
        to_south = jnp.where(row_at == 0, bottom, pltpu.roll(here, 1, 0))
        here, to_east, to_west, to_north, to_south = (
            value[:, :cols] for value in (here, to_east, to_west, to_north, to_south))
        return (-0.5 * zc[level] * (to_east - to_west)
                - 0.5 * nc[level] * (to_north - to_south)
                + DIFFUSION * (to_east + to_west + to_north + to_south - 4.0 * here))

    q[:, :, (width - LANES):] = jnp.zeros((levels, rows, LANES), F32)
    loads[0].wait()
    for load in loads[1:]:
        load.start()
    for level in range(levels):
        q[level, :, :cols] = q_in[level]
    pack_rows(0)
    pack_cols(0)

    ends = first.astype(jnp.int32) + last.astype(jnp.int32)
    sides = jnp.where(polar, lon_count - 1, 2)
    pl.semaphore_wait(barrier, 2 - ends + sides)

    @pl.when(jnp.logical_not(last))
    def _():
        row_copy(0, 0).start()

    @pl.when(jnp.logical_not(first))
    def _():
        row_copy(0, 1).start()

    @pl.when(last)
    def _():
        pole_copy(0).start()

    @pl.when(first)
    def _():
        pole_copy(1).start()

    col_copy(0, 0).start()
    col_copy(0, 1).start()

    offset = jnp.where(
        lat < cap_blocks, lat * rows,
        jnp.where(polar, (lat - lat_count + 2 * cap_blocks) * rows, 0))
    tend[...] = jnp.zeros_like(tend)
    for load in loads[1:]:
        load.wait()

    @pl.when(jnp.logical_not(last))
    def _():
        row_copy(0, 1).wait_recv()
        row_copy(0, 0).wait_send()

    @pl.when(jnp.logical_not(first))
    def _():
        row_copy(0, 0).wait_recv()
        row_copy(0, 1).wait_send()

    @pl.when(last)
    def _():
        pole_copy(0).wait()
        row_in[0, 1] = pole_in[...]

    @pl.when(first)
    def _():
        pole_copy(1).wait()
        row_in[0, 0] = pole_in[...]

    col_copy(0, 0).wait()
    col_copy(0, 1).wait()
    place_cols(0)

    @pl.when(jnp.logical_not(polar))
    def _():
        for level in range(levels):
            tend[level, :, :cols] = stencil(0, level)
        for level in range(levels):
            q[level, :, :cols] = q[level, :, :cols] + tend[level, :, :cols]
        pack_rows(1)
        row_copy(1, 0).start()
        row_copy(1, 1).start()
        pack_cols(1)
        col_copy(1, 0).start()
        col_copy(1, 1).start()
        row_copy(1, 0).wait()
        row_copy(1, 1).wait()
        col_copy(1, 0).wait()
        col_copy(1, 1).wait()
        place_cols(1)
        for level in range(levels):
            out[level] = q[level, :, :cols] + stencil(1, level)

    @pl.when(polar)
    def _():
        mode = lax.broadcasted_iota(jnp.int32, (rows, KMAX), 1)
        which = lax.broadcasted_iota(jnp.int32, (rows, KMAX), 0)
        weight = jnp.where(mode == 0, 1.0 / total, 2.0 / total).astype(F32)
        cut = jnp.zeros((rows, KMAX), jnp.int32)
        for row in range(rows):
            cut = jnp.where(which == row, cut_ref[offset + row], cut)
        keep = jnp.where(mode < cut, weight, 0.0)[None]
        cosine = phase[0:1, :]
        sine = phase[1:2, :]
        parity = 1.0 - 2.0 * (lax.broadcasted_iota(jnp.int32, (1, 2 * KMAX), 1) % 2).astype(F32)

        def analyse(turn, piece):
            here = slice(piece * per, (piece + 1) * per)
            for level in range(piece * per, (piece + 1) * per):
                tend[level, :, :cols] = stencil(turn, level)
            partial = dot3(tend[here].reshape(per * rows, width), ana)
            real = partial[:, :KMAX]
            imag = partial[:, KMAX:]
            part[turn, here, :, :KMAX] = (real * cosine - imag * sine).reshape(per, rows, KMAX)
            part[turn, here, :, KMAX:] = (real * sine + imag * cosine).reshape(per, rows, KMAX)
            send_sums(turn, piece)

        def collect(turn, piece):
            here = slice(piece * per, (piece + 1) * per)
            for step in range(1, lon_count):
                sum_arrival(turn, piece, lax.rem(lon + step, lon_count)).wait_recv()
            summed = part[turn, here]
            for step in range(1, lon_count):
                summed = summed + part_in[turn, lax.rem(lon + step, lon_count), here]
            real = (summed[:, :, :KMAX] * keep).reshape(per * rows, KMAX)
            imag = (summed[:, :, KMAX:] * keep).reshape(per * rows, KMAX)
            return jnp.concatenate(
                [real * cosine + imag * sine, imag * cosine - real * sine], axis=1)

        def sums_sent(turn):
            for piece in range(PIECES):
                for step in range(1, lon_count):
                    sum_copy(turn, piece, lax.rem(lon + step, lon_count)).wait_send()

        for piece in range(PIECES):
            analyse(0, piece)
        pole_rows = []
        for piece in range(PIECES):
            here = slice(piece * per, (piece + 1) * per)
            local = collect(0, piece)
            q[here] = q[here] + dot3(local, syn).reshape(per, rows, width)
            local = local.reshape(per, rows, 2 * KMAX)
            pole_rows.append(jnp.where(first, local[:, 0, :], local[:, rows - 1, :]))
        pack_rows(1)

        @pl.when(jnp.logical_not(last))
        def _():
            row_copy(1, 0).start()

        @pl.when(jnp.logical_not(first))
        def _():
            row_copy(1, 1).start()

        pole_row = jnp.concatenate(pole_rows, axis=0) * parity
        pole_sum = pole_in[...] + dot3(pole_row, syn)

        @pl.when(last)
        def _():
            row_in[1, 1] = pole_sum

        @pl.when(first)
        def _():
            row_in[1, 0] = pole_sum

        @pl.when(jnp.logical_not(last))
        def _():
            row_copy(1, 1).wait_recv()
            row_copy(1, 0).wait_send()

        @pl.when(jnp.logical_not(first))
        def _():
            row_copy(1, 0).wait_recv()
            row_copy(1, 1).wait_send()

        for piece in range(PIECES):
            analyse(1, piece)
        for piece in range(PIECES):
            filtered = dot3(collect(1, piece), syn).reshape(per, rows, width)
            for level in range(per):
                there = piece * per + level
                out[there] = q[there, :, :cols] + filtered[level, :, :cols]
        sums_sent(0)
        sums_sent(1)


def shards(tracer, zonal_courant, north_courant, cutoff):
    levels, rows, cols = tracer.shape
    lat_count = lax.axis_size("lat")
    lon_count = lax.axis_size("lon")
    cap_blocks = lat_count // 8
    width = -(-(cols + 2) // LANES) * LANES
    analysis, synthesis, phase = tables(cols, width, lon_count)
    dma = pltpu.SemaphoreType.DMA
    anywhere = pl.BlockSpec(memory_space=pl.ANY)
    return pl.pallas_call(
        functools.partial(kernel, lat_count, lon_count, cap_blocks),
        out_shape=pltpu.VMEM(tracer.shape, F32),
        in_specs=[pl.BlockSpec(memory_space=pltpu.SMEM)] + [anywhere] * 6,
        out_specs=pl.BlockSpec(memory_space=pltpu.VMEM),
        scratch_shapes=[
            pltpu.VMEM((levels, rows, cols), F32),
            pltpu.VMEM((levels, rows, cols), F32),
            pltpu.VMEM((levels, rows, cols), F32),
            pltpu.VMEM(analysis.shape, BF16),
            pltpu.VMEM(synthesis.shape, BF16),
            pltpu.VMEM(phase.shape[1:], F32),
            pltpu.VMEM((levels, rows, width), F32),
            pltpu.VMEM((levels, rows, width), F32),
            pltpu.VMEM((2, 2, levels, width), F32),
            pltpu.VMEM((2, 2, levels, width), F32),
            pltpu.VMEM((2, 2, rows, LANES), F32),
            pltpu.VMEM((2, 2, rows, LANES), F32),
            pltpu.VMEM((levels, width), F32),
            pltpu.VMEM((2, levels, rows, 2 * KMAX), F32),
            pltpu.VMEM((2, lon_count, levels, rows, 2 * KMAX), F32),
            dma((6,)),
            dma((2, 2)), dma((2, 2)), dma((2, 2)), dma((2, 2)),
            dma(()), dma(()),
            dma((2, PIECES, lon_count)), dma((2, PIECES, lon_count)),
        ],
        compiler_params=pltpu.CompilerParams(collective_id=0, has_side_effects=True),
    )(cutoff, tracer, zonal_courant, north_courant,
      jnp.asarray(analysis), jnp.asarray(synthesis), jnp.asarray(phase))


def solution(mesh):
    return jax.shard_map(
        shards,
        mesh=mesh,
        in_specs=(P(None, "lat", "lon"), P(None, "lat", "lon"), P(None, "lat", "lon"), P()),
        out_specs=P(None, "lat", "lon"),
        check_vma=False,
    )
```

```python
import functools
import math

import jax
import jax.numpy as jnp
import numpy as np
from jax import lax
from jax.experimental import pallas as pl
from jax.experimental.pallas import tpu as pltpu
from jax.sharding import PartitionSpec as P

KMAX = 128
DIFFUSION = 0.2
LANES = 128
MESH = pl.DeviceIdType.MESH
F32 = jnp.float32
BF16 = jnp.bfloat16


def split_table(table):
    high = table.astype(np.float32).astype(BF16)
    low = (table - high.astype(np.float64)).astype(np.float32).astype(BF16)
    return np.stack([high, low])


def trig(columns, total):
    modes = np.arange(KMAX)
    angle = (columns[:, None] * modes[None, :] % total) * (2.0 * math.pi / total)
    return np.concatenate([np.cos(angle), np.sin(angle)], axis=1)


def tables(cols, width, lon_count):
    lane = np.arange(width)
    lane = np.where(lane == width - 1, -1, lane)
    total = cols * lon_count
    both = trig(lane, total)
    ends = np.zeros((lon_count, 8, 2 * KMAX), np.float32)
    ends[:, 0] = trig(np.arange(lon_count) * cols, total)
    ends[:, 1] = trig(np.arange(lon_count) * cols + cols - 1, total)
    return split_table(both), split_table(both.T.copy()), ends


def split(value):
    high = value.astype(BF16)
    low = (value - high.astype(F32)).astype(BF16)
    return high, low


def dot3(value, table):
    high, low = split(value)
    t_high = table[0]
    t_low = table[1]
    dot = functools.partial(jnp.dot, preferred_element_type=F32)
    return dot(high, t_high) + (dot(low, t_high) + dot(high, t_low))


def kernel(
    lat_count, lon_count, cap_blocks,
    cut_ref, tracer, zonal, north, ana_hbm, syn_hbm, ends_hbm, out,
    q_in, zc, nc, ana, syn, ends, q, tend,
    row_first, row_second, col_out, col_in, part, part_in, extra,
    load_sem, row_send, row_recv, col_send, col_recv, sum_send, sum_recv,
):
    rows, levels, cols = q_in.shape
    width = q.shape[2]
    total = cols * lon_count
    lat = lax.axis_index("lat")
    lon = lax.axis_index("lon")
    polar = jnp.logical_or(lat < cap_blocks, lat >= lat_count - cap_blocks)
    first = lat == 0
    last = lat == lat_count - 1
    east = lax.rem(lon + 1, lon_count)
    west = lax.rem(lon + lon_count - 1, lon_count)
    across = lax.rem(lon + lon_count // 2, lon_count)
    peers = [lax.rem(lon + step, lon_count) for step in range(1, lon_count)]
    order = [0, rows - 1, 1, rows - 2] + list(range(2, rows - 2))
    pieces = (((2, rows), (0, 2)), ((4, rows), (0, 4)))

    loads = []
    for index, (source, target) in enumerate(((tracer, q_in), (zonal, zc), (north, nc))):
        for row in range(rows):
            loads.append(pltpu.make_async_copy(
                source.at[:, row, :], target.at[row], load_sem.at[index * rows + row]))
    for load in loads[:rows]:
        load.start()

    barrier = pltpu.get_barrier_semaphore()

    def greet(there):
        pl.semaphore_signal(barrier, inc=1, device_id=there, device_id_type=MESH)

    @pl.when(jnp.logical_not(first))
    def _():
        greet({"lat": lat - 1, "lon": lon})

    @pl.when(jnp.logical_not(last))
    def _():
        greet({"lat": lat + 1, "lon": lon})

    @pl.when(polar)
    def _():
        for peer in peers:
            greet({"lat": lat, "lon": peer})

    @pl.when(jnp.logical_not(polar))
    def _():
        greet({"lat": lat, "lon": east})
        greet({"lat": lat, "lon": west})

    for load in loads[rows:]:
        load.start()
    tables_in = [
        pltpu.make_async_copy(ana_hbm, ana, load_sem.at[3 * rows]),
        pltpu.make_async_copy(syn_hbm, syn, load_sem.at[3 * rows + 1]),
        pltpu.make_async_copy(ends_hbm, ends, load_sem.at[3 * rows + 2]),
    ]
    for load in tables_in:
        load.start()

    edge = first.astype(jnp.int32) + last.astype(jnp.int32)
    sides = jnp.where(polar, lon_count - 1, 2)
    pl.semaphore_wait(barrier, 2 - edge + sides)

    def row_copy(turn, slot, row, there):
        source = tracer.at[:, row, :] if turn == 0 else q.at[row]
        target = row_first if turn == 0 else row_second
        return pltpu.make_async_remote_copy(
            source, target.at[slot],
            row_send.at[turn, 0 if row else 1], row_recv.at[turn, slot],
            device_id=there, device_id_type=MESH)

    def to_north(turn):
        return row_copy(turn, 0, rows - 1, {"lat": lat + 1, "lon": lon})

    def to_south(turn):
        return row_copy(turn, 1, 0, {"lat": lat - 1, "lon": lon})

    def over_north():
        return row_copy(0, 1, rows - 1, {"lat": lat, "lon": across})

    def over_south():
        return row_copy(0, 0, 0, {"lat": lat, "lon": across})

    @pl.when(last)
    def _():
        over_north().start()

    @pl.when(first)
    def _():
        over_south().start()

    @pl.when(jnp.logical_not(last))
    def _():
        to_north(0).start()

    @pl.when(jnp.logical_not(first))
    def _():
        to_south(0).start()

    def rows_arrive(turn):
        @pl.when(jnp.logical_not(last))
        def _():
            to_south(turn).wait_recv()
            to_north(turn).wait_send()

        @pl.when(jnp.logical_not(first))
        def _():
            to_north(turn).wait_recv()
            to_south(turn).wait_send()

    def poles_arrive():
        @pl.when(last)
        def _():
            over_north().wait()

        @pl.when(first)
        def _():
            over_south().wait()

    lane = lax.broadcasted_iota(jnp.int32, (levels, LANES), 1)
    end_tile = (cols - 1) // LANES * LANES
    end_lane = (cols - 1) % LANES
    east_tile = cols // LANES * LANES
    west_tile = width - LANES

    def pack_cols(turn):
        packed = jnp.zeros((levels, LANES), F32)

        def put(packed, at, tile, came_from):
            return jnp.where(lane == at, pltpu.roll(tile, (at - came_from) % LANES, 1), packed)

        for row in range(rows):
            packed = put(packed, row, q[row, :, end_tile:end_tile + LANES], end_lane)
            packed = put(packed, rows + row, q[row, :, 0:LANES], 0)
        return packed

    def pack_factors(packed):
        for row in range(rows):
            tile = zc[row, :, end_tile:cols]
            if cols - end_tile < LANES:
                tile = jnp.concatenate(
                    [tile, jnp.zeros((levels, LANES - cols + end_tile), F32)], axis=1)
            factor = DIFFUSION - 0.5 * tile
            packed = jnp.where(
                lane == 2 * rows + row,
                pltpu.roll(factor, (2 * rows + row - end_lane) % LANES, 1), packed)
            factor = DIFFUSION + 0.5 * zc[row, :, 0:LANES]
            packed = jnp.where(
                lane == 3 * rows + row, pltpu.roll(factor, 3 * rows + row, 1), packed)
        return packed

    def place_cols(turn):
        from_west = col_in[turn, west]
        from_east = col_in[turn, east]
        for row in range(rows):
            tile = q[row, :, east_tile:east_tile + LANES]
            moved = pltpu.roll(from_east, (cols % LANES - rows - row) % LANES, 1)
            q[row, :, east_tile:east_tile + LANES] = jnp.where(lane == cols % LANES, moved, tile)
            tile = q[row, :, west_tile:west_tile + LANES]
            moved = pltpu.roll(from_west, (LANES - 1 - row) % LANES, 1)
            q[row, :, west_tile:west_tile + LANES] = jnp.where(lane == LANES - 1, moved, tile)

    def col_copy(turn, target):
        return pltpu.make_async_remote_copy(
            col_out.at[turn], col_in.at[turn, lon],
            col_send.at[turn, target], col_recv.at[turn, lon],
            device_id={"lat": lat, "lon": target}, device_id_type=MESH)

    def col_arrival(turn, source):
        theirs = col_in.at[turn, source]
        return pltpu.make_async_remote_copy(
            theirs, theirs, col_send.at[turn, source], col_recv.at[turn, source],
            device_id={"lat": lat, "lon": source}, device_id_type=MESH)

    def sum_copy(turn, piece, target):
        low, high = pieces[turn][piece]
        return pltpu.make_async_remote_copy(
            part.at[turn, low:high], part_in.at[turn, lon, low:high],
            sum_send.at[turn, piece, target], sum_recv.at[turn, piece, lon],
            device_id={"lat": lat, "lon": target}, device_id_type=MESH)

    def sum_arrival(turn, piece, source):
        low, high = pieces[turn][piece]
        theirs = part_in.at[turn, source, low:high]
        return pltpu.make_async_remote_copy(
            theirs, theirs, sum_send.at[turn, piece, source], sum_recv.at[turn, piece, source],
            device_id={"lat": lat, "lon": source}, device_id_type=MESH)

    def farthest_first(send):
        for distance in range(lon_count - 1, 0, -1):
            @pl.when(lon + distance < lon_count)
            def _():
                send(lon + distance)

            @pl.when(lon - distance >= 0)
            def _():
                send(lon - distance)

    def stencil(turn, row):
        beyond = row_first if turn == 0 else row_second
        here = q[row]
        to_east = pltpu.roll(here, width - 1, 1)[:, :cols]
        to_west = pltpu.roll(here, 1, 1)[:, :cols]
        here = here[:, :cols]
        up = q[row + 1, :, :cols] if row < rows - 1 else beyond[1, :, :cols]
        down = q[row - 1, :, :cols] if row else beyond[0, :, :cols]
        return (-0.5 * zc[row] * (to_east - to_west)
                - 0.5 * nc[row] * (up - down)
                + DIFFUSION * (to_east + to_west + up + down - 4.0 * here))

    q[:, :, (width - LANES):] = jnp.zeros((rows, levels, LANES), F32)
    for load in loads[:rows]:
        load.wait()
    for row in range(rows):
        q[row, :, :cols] = q_in[row]

    @pl.when(jnp.logical_not(polar))
    def _():
        col_out[0] = pack_cols(0)
        for side in (east, west):
            col_copy(0, side).start()
        for load in loads[rows:] + tables_in:
            load.wait()
        for side in (east, west):
            col_arrival(0, side).wait_recv()
        place_cols(0)
        rows_arrive(0)
        for row in range(rows):
            tend[row, :, :cols] = stencil(0, row)
        for row in range(rows):
            q[row, :, :cols] = q[row, :, :cols] + tend[row, :, :cols]
        to_north(1).start()
        to_south(1).start()
        col_out[1] = pack_cols(1)
        for side in (east, west):
            col_copy(1, side).start()
        for side in (east, west):
            col_arrival(1, side).wait_recv()
        rows_arrive(1)
        place_cols(1)
        for row in range(rows):
            out[:, row, :] = q[row, :, :cols] + stencil(1, row)
        for turn in range(2):
            for side in (east, west):
                col_copy(turn, side).wait_send()

    @pl.when(polar)
    def _():
        tend[:, :, (width - LANES):] = jnp.zeros((rows, levels, LANES), F32)
        for load in loads[rows:2 * rows]:
            load.wait()
        col_out[0] = pack_factors(pack_cols(0))
        farthest_first(lambda target: col_copy(0, target).start())
        for load in loads[2 * rows:] + tables_in:
            load.wait()

        cosine = ends[lon, 0:1, :KMAX]
        sine = ends[lon, 0:1, KMAX:]
        offset = jnp.where(
            lat < cap_blocks, lat * rows, (lat - lat_count + 2 * cap_blocks) * rows)
        mode = lax.broadcasted_iota(jnp.int32, (1, KMAX), 1)
        weight = jnp.where(mode == 0, 1.0 / total, 2.0 / total).astype(F32)
        keep = [jnp.where(mode < cut_ref[offset + row], weight, 0.0) for row in range(rows)]
        parity = 1.0 - 2.0 * (lax.broadcasted_iota(jnp.int32, (1, 2 * KMAX), 1) % 2).astype(F32)

        def analyse(turn, piece):
            low, high = pieces[turn][piece]
            count = high - low
            for slot in range(low, high):
                tend[slot, :, :cols] = stencil(turn, order[slot])
            partial = dot3(tend[low:high].reshape(count * levels, width), ana)
            real = partial[:, :KMAX]
            imag = partial[:, KMAX:]
            part[turn, low:high, :, :KMAX] = (real * cosine - imag * sine).reshape(count, levels, KMAX)
            part[turn, low:high, :, KMAX:] = (real * sine + imag * cosine).reshape(count, levels, KMAX)
            farthest_first(lambda target: sum_copy(turn, piece, target).start())

        def collect(turn, piece):
            low, high = pieces[turn][piece]
            for peer in peers:
                sum_arrival(turn, piece, peer).wait_recv()
            result = []
            for slot in range(low, high):
                summed = part[turn, slot]
                if turn == 0:
                    summed = summed + extra[slot]
                for peer in peers:
                    summed = summed + part_in[turn, peer, slot]
                real = summed[:, :KMAX] * keep[order[slot]]
                imag = summed[:, KMAX:] * keep[order[slot]]
                result.append(jnp.concatenate(
                    [real * cosine + imag * sine, imag * cosine - real * sine], axis=1))
            return result

        def synthesise(parts):
            return dot3(jnp.concatenate(parts, axis=0), syn).reshape(len(parts), levels, width)

        analyse(0, 0)
        rows_arrive(0)
        poles_arrive()
        analyse(0, 1)

        for peer in peers:
            col_arrival(0, peer).wait_recv()
        col_in[0, lon] = col_out[0]
        place_cols(0)
        packed = [col_in[0, place] for place in range(lon_count)]
        added = [jnp.zeros((levels, 2 * KMAX), F32) for _ in range(rows)]
        for place in range(lon_count):
            behind = packed[place - 1]
            ahead = packed[(place + 1) % lon_count]
            at_last = packed[place] * pltpu.roll(ahead, rows, 1)
            at_first = packed[place] * pltpu.roll(behind, 3 * rows, 1)
            for row in range(rows):
                column = at_last[:, 2 * rows + row:2 * rows + row + 1]
                added[row] = added[row] + column * ends[place, 1:2, :]
                column = at_first[:, 3 * rows + row:3 * rows + row + 1]
                added[row] = added[row] + column * ends[place, 0:1, :]
        for slot in range(rows):
            extra[slot] = added[order[slot]]

        low, high = pieces[0][0]
        filtered = synthesise(collect(0, 0))
        for slot in range(low, high):
            q[order[slot]] = q[order[slot]] + filtered[slot - low]
        analyse(1, 0)

        local = collect(0, 1)
        pole_row = jnp.where(first, local[0], local[1]) * parity
        filtered = synthesise(local + [pole_row])
        q[0] = q[0] + filtered[0]
        q[rows - 1] = q[rows - 1] + filtered[1]

        @pl.when(jnp.logical_not(last))
        def _():
            to_north(1).start()

        @pl.when(jnp.logical_not(first))
        def _():
            to_south(1).start()

        @pl.when(last)
        def _():
            row_second[1, :, :cols] = row_first[1] + filtered[2, :, :cols]

        @pl.when(first)
        def _():
            row_second[0, :, :cols] = row_first[0] + filtered[2, :, :cols]

        rows_arrive(1)
        analyse(1, 1)
        for piece in range(2):
            low, high = pieces[1][piece]
            filtered = synthesise(collect(1, piece))
            for slot in range(low, high):
                row = order[slot]
                out[:, row, :] = q[row, :, :cols] + filtered[slot - low, :, :cols]
        for peer in peers:
            col_copy(0, peer).wait_send()
            for turn in range(2):
                for piece in range(2):
                    sum_copy(turn, piece, peer).wait_send()


def shards(tracer, zonal_courant, north_courant, cutoff):
    levels, rows, cols = tracer.shape
    lat_count = lax.axis_size("lat")
    lon_count = lax.axis_size("lon")
    cap_blocks = lat_count // 8
    width = -(-(cols + 2) // LANES) * LANES
    analysis, synthesis, ends = tables(cols, width, lon_count)
    dma = pltpu.SemaphoreType.DMA
    anywhere = pl.BlockSpec(memory_space=pl.ANY)
    return pl.pallas_call(
        functools.partial(kernel, lat_count, lon_count, cap_blocks),
        out_shape=pltpu.VMEM(tracer.shape, F32),
        in_specs=[pl.BlockSpec(memory_space=pltpu.SMEM)] + [anywhere] * 6,
        out_specs=pl.BlockSpec(memory_space=pltpu.VMEM),
        scratch_shapes=[
            pltpu.VMEM((rows, levels, cols), F32),
            pltpu.VMEM((rows, levels, cols), F32),
            pltpu.VMEM((rows, levels, cols), F32),
            pltpu.VMEM(analysis.shape, BF16),
            pltpu.VMEM(synthesis.shape, BF16),
            pltpu.VMEM(ends.shape, F32),
            pltpu.VMEM((rows, levels, width), F32),
            pltpu.VMEM((rows, levels, width), F32),
            pltpu.VMEM((2, levels, cols), F32),
            pltpu.VMEM((2, levels, width), F32),
            pltpu.VMEM((2, levels, LANES), F32),
            pltpu.VMEM((2, lon_count, levels, LANES), F32),
            pltpu.VMEM((2, rows, levels, 2 * KMAX), F32),
            pltpu.VMEM((2, lon_count, rows, levels, 2 * KMAX), F32),
            pltpu.VMEM((rows, levels, 2 * KMAX), F32),
            dma((3 * rows + 3,)),
            dma((2, 2)), dma((2, 2)), dma((2, lon_count)), dma((2, lon_count)),
            dma((2, 2, lon_count)), dma((2, 2, lon_count)),
        ],
        compiler_params=pltpu.CompilerParams(collective_id=0, has_side_effects=True),
    )(cutoff, tracer, zonal_courant, north_courant,
      jnp.asarray(analysis), jnp.asarray(synthesis), jnp.asarray(ends))


def solution(mesh):
    return jax.shard_map(
        shards,
        mesh=mesh,
        in_specs=(P(None, "lat", "lon"), P(None, "lat", "lon"), P(None, "lat", "lon"), P()),
        out_specs=P(None, "lat", "lon"),
        check_vma=False,
    )
```
